256 devices in a mesh: pb: 32 (over x, y, z_lo), row: 8 (over z_hi, core).
Axes of the slice: x: 4, y: 4, z: 8 (z_hi: 4, z_lo: 2; z = z_hi * 2 + z_lo), core: 2. Of those that a mesh axis runs over, the one named last changes fastest.
Arguments:
- query_desc: bfloat16 [16384, 512], P(('pb', 'row')), may hold values from -6 to 6
- ref_desc: bfloat16 [12288, 512], P(('row', 'pb')), may hold values from -6 to 6
- taps: float32 [2, 8], replicated, may hold values from -1.3 to 1.3
Outputs:
- aligned: float32 [16384, 12288], P('pb', 'row')
The draws below stay inside these ranges and needn't reach their ends.
All inputs are finite; a program needn't handle non-finite values.
Results may differ from the reference program's by a relative error of at most 0.0003.
Values may be sent and summed in bfloat16 or wider, within the bound.
No kernel may reach another device: no remote copies, remote signals or barrier semaphores. Data moves between devices by JAX's collectives and lax.ppermute only.
A program may use at most 64 MiB of HBM per device.

```python
import jax
import jax.numpy as jnp
from jax import lax

DESC = 512
QF_DEV = 512
DILATION_STEP = 32
TAP_COUNT = 8
NQ = 16384
NR = 12288


def levels(stream_key, extent, split, low, top_value):
    factor_of, own = 1.0, jax.random.fold_in(stream_key, 6)
    for position, blocks in split:
        steps = jnp.exp(jax.random.uniform(jax.random.fold_in(own, position), (blocks,), jnp.float32, low / len(split), top_value / len(split)))
        factor_of = factor_of * jnp.repeat(steps, extent[position] // blocks).reshape([-1 if axis == position else 1 for axis in range(len(extent))])
    return factor_of


def bell_draw(key, extent, scale, bound, shards=(), held_as=jnp.bfloat16):
    factor_of = levels(key, extent, shards, -0.22, 0.18) if shards else 1.0
    values = jax.random.normal(key, extent, jnp.float32) * scale * factor_of
    return jnp.minimum(jnp.maximum(values, -bound), bound).astype(held_as)


def setup_inputs(seed: int = 0) -> dict:
    arg_keys = jax.random.split(jax.random.key(seed), 4)
    return {
        "query_desc": bell_draw(arg_keys[0], (NQ, DESC), 1.0, 6.0, ((0, 256),)),
        "ref_desc": bell_draw(arg_keys[1], (NR, DESC), 1.0, 6.0, ((0, 256),)),
        "taps": bell_draw(arg_keys[2], (2, TAP_COUNT), 0.45, 1.3, (), jnp.float32),
    }


def diagonal_pass(padded_matrix, tap_weights, output_rows, output_columns):
    total_reach = jnp.zeros((output_rows, output_columns), jnp.float32)
    for tap_index in range(TAP_COUNT):
        total_reach = total_reach + tap_weights[tap_index] * padded_matrix[tap_index * DILATION_STEP:tap_index * DILATION_STEP + output_rows, tap_index * DILATION_STEP:tap_index * DILATION_STEP + output_columns]
    return jnp.tanh(total_reach)


def reference(query_desc, ref_desc, taps):
    border_margin = TAP_COUNT * DILATION_STEP
    half_extent = TAP_COUNT * DILATION_STEP // 2
    scale = DESC ** -0.5
    query_pad = jnp.pad(query_desc, ((border_margin, border_margin), (0, 0)))
    ref_pad = jnp.pad(ref_desc, ((border_margin, border_margin), (0, 0)))
    blocks = NQ // QF_DEV

    def one_block(index):
        rows = lax.dynamic_slice_in_dim(query_pad, index * QF_DEV, QF_DEV + 2 * border_margin, 0)
        sim = jnp.dot(rows, ref_pad.T, preferred_element_type=jnp.float32) * scale
        base = jnp.tanh(sim)
        first = diagonal_pass(base, taps[0], QF_DEV + 2 * half_extent, NR + 2 * half_extent)
        row_ids = index * QF_DEV + jnp.arange(QF_DEV + 2 * half_extent, dtype=jnp.int32) - half_extent
        col_ids = jnp.arange(NR + 2 * half_extent, dtype=jnp.int32) - half_extent
        row_ok = ((row_ids >= 0) & (row_ids < NQ)).astype(jnp.float32)
        col_ok = ((col_ids >= 0) & (col_ids < NR)).astype(jnp.float32)
        first = first * row_ok[:, None] * col_ok[None, :]
        return diagonal_pass(first, taps[1], QF_DEV, NR)

    stacked = lax.map(one_block, jnp.arange(blocks, dtype=jnp.int32))
    return stacked.reshape(NQ, NR)
```

```python
import jax
import jax.numpy as jnp
import numpy as np
from jax import lax
from jax.experimental import pallas as pl
from jax.experimental.pallas import tpu as pltpu
from jax.sharding import Mesh, PartitionSpec as P

D = 32
K = 8
DESC = 512
NB = 30
TW = 17 * 128


def kernel(mine_ref, other_ref, refs_ref, left_ref, right_ref, taps_ref, flag_ref, place_ref,
           o_ref, qs, rs, base, res, cmask):
    scale = DESC ** -0.5
    zh, core = place_ref[0], place_ref[1]
    for s in range(4):
        for ref, c in ((mine_ref, core), (other_ref, 1 - core)):
            w = 2 * lax.rem(zh - s + 4, 4) + c
            qs[pl.ds(pl.multiple_of(256 + w * 64, 64), 64), :] = ref[s * 128:s * 128 + 64, :]
            rim = jnp.where(w >= 4, (w - 4) * 64, 768 + w * 64)
            qs[pl.ds(pl.multiple_of(rim, 64), 64), :] = ref[s * 128 + 64:s * 128 + 128, :]
    rs[0:128, :] = jnp.zeros((128, DESC), rs.dtype)
    rs[2112:2304, :] = jnp.zeros((192, DESC), rs.dtype)
    rs[128:384, :] = left_ref[...]
    rs[384:1920, :] = refs_ref[...]
    rs[1920:2112, :] = right_ref[...]

    for c in range(4):
        us = list(range(c, NB, 4))
        lhs = jnp.concatenate([qs[u * D:(u + 1) * D, :] for u in us], axis=0)

        def col(t, _, us=us, lhs=lhs, c=c):
            rhs = rs[pl.ds(pl.multiple_of(t * 128 + c * D, D), 128), :]
            s = lax.dot_general(lhs, rhs, (((1,), (1,)), ((), ())), preferred_element_type=jnp.float32)
            s = jnp.tanh(s * scale)
            for n, u in enumerate(us):
                base[u * D:(u + 1) * D, pl.ds(pl.multiple_of(t * 128, 128), 128)] = s[n * D:(n + 1) * D]
            return 0

        lax.fori_loop(0, 17, col, 0)
        j = lax.broadcasted_iota(jnp.int32, (8, TW), 1) + (c * D - 128)
        cmask[c * 8:(c + 1) * 8, :] = jnp.where(j < 256, flag_ref[2], jnp.where(j >= 1792, flag_ref[3], 1.0))
    w0 = [taps_ref[0, k] for k in range(K)]
    w1 = [taps_ref[1, k] for k in range(K)]

    def tap_sum(w, vals):
        p = [a * b for a, b in zip(w, vals)]
        while len(p) > 1:
            p = [p[i] + p[i + 1] for i in range(0, len(p), 2)]
        return p[0]

    def chain(m, v, lo, hi):
        def rows(u):
            return pl.ds(pl.multiple_of(u * D + v * 8, 8), 8)

        def lanes(u):
            return pl.ds(pl.multiple_of((m + u // 4 + 1) * 128, 128), 128)

        d = {u: base[rows(u), lanes(u)] for u in range(lo - 8, hi + 7)}
        f = {}
        for u in range(lo - 4, hi + 4):
            x = jnp.tanh(tap_sum(w0, [d[u + k - 4] for k in range(K)]))
            x = x * cmask[(u % 4) * 8:(u % 4) * 8 + 8, lanes(u)]
            if u < 8:
                x = x * flag_ref[0]
            if u >= 24:
                x = x * flag_ref[1]
            f[u] = x
        for u in range(lo, hi + 1):
            res[rows(u - 8), lanes(u)] = jnp.tanh(tap_sum(w1, [f[u + k - 4] for k in range(K)]))

    def diagonals(m0, m1, lo, hi):
        def step(i, _):
            chain(m0 + i // 4, lax.rem(i, 4), lo, hi)
            return 0

        lax.fori_loop(0, 4 * (m1 - m0), step, 0)

    diagonals(-1, 9, 8, 23)
    diagonals(-4, -3, 20, 23)
    diagonals(-3, -2, 16, 23)
    diagonals(-2, -1, 12, 23)
    diagonals(9, 10, 8, 19)
    diagonals(10, 11, 8, 15)
    diagonals(11, 12, 8, 11)
    for b in range(16):
        s = 384 - 32 * (b % 4)
        o_ref[b * D:(b + 1) * D, :] = res[b * D:(b + 1) * D, s:s + 1536]


def tile(*args):
    vmem, smem = pl.BlockSpec(memory_space=pltpu.VMEM), pl.BlockSpec(memory_space=pltpu.SMEM)
    return pl.pallas_call(
        kernel,
        out_shape=jax.ShapeDtypeStruct((512, 1536), jnp.float32),
        in_specs=[vmem] * 5 + [smem] * 3,
        out_specs=vmem,
        scratch_shapes=[
            pltpu.VMEM((1024, DESC), jnp.bfloat16),
            pltpu.VMEM((2304, DESC), jnp.bfloat16),
            pltpu.VMEM((NB * D, TW), jnp.float32),
            pltpu.VMEM((512, TW), jnp.float32),
            pltpu.VMEM((32, TW), jnp.float32),
        ],
        compiler_params=pltpu.CompilerParams(vmem_limit_bytes=40 << 20),
        cost_estimate=pl.CostEstimate(flops=2 * 960 * 1984 * 512, bytes_accessed=6 << 20, transcendentals=0),
    )(*args)


def grid_perm(sizes, move):
    pairs = []
    for src in np.ndindex(*sizes):
        dst = move(*src)
        if dst is not None:
            pairs.append((int(np.ravel_multi_index(src, sizes)), int(np.ravel_multi_index(dst, sizes))))
    return pairs


PB = ("x", "y", "zl")
ROW = ("zh", "c")
SIZES = (4, 4, 2, 4, 2)


def local(q, r, taps):
    pb, row = lax.axis_index(PB), lax.axis_index(ROW)

    def halo_move(x, y, zl, zh, c):
        p, w = (x * 4 + y) * 2 + zl, zh * 2 + c
        p = p + 1 if w >= 4 else p - 1
        if p < 0 or p > 31:
            return None
        return (p // 8, p // 2 % 4, p % 2, zh, c)

    halo = lax.ppermute(q, PB + ROW, grid_perm(SIZES, halo_move))
    both = jnp.concatenate([q, halo], axis=0)
    zh = lax.axis_index("zh")
    shifted = [lax.ppermute(both, "zh", [(i, (i + d) % 4) for i in range(4)]) for d in (1, 2, 3)]
    stack = jnp.concatenate([both] + shifted, axis=0)
    other = lax.ppermute(stack, "c", [(0, 1), (1, 0)])

    refs = lax.all_to_all(jnp.broadcast_to(r[None], (32, 48, DESC)), PB, 0, 0, tiled=True).reshape(1536, DESC)
    left = lax.ppermute(refs[1280:], ROW, [(i, i + 1) for i in range(7)])
    right = lax.ppermute(refs[:192], ROW, [(i + 1, i) for i in range(7)])
    flags = jnp.stack([pb != 0, pb != 31, row != 0, row != 7]).astype(jnp.float32)
    place = jnp.stack([zh, lax.axis_index("c")])
    return tile(stack, other, refs, left, right, taps, flags, place)


def solution(mesh):
    split = Mesh(mesh.devices.reshape(SIZES), PB + ROW)
    specs = (P(PB + ROW, None), P(ROW + PB, None), P())
    return jax.shard_map(local, mesh=split, in_specs=specs, out_specs=P(PB, ROW), check_vma=False)
```

```python
import jax
import jax.numpy as jnp
import numpy as np
from jax import lax
from jax.experimental import pallas as pl
from jax.experimental.pallas import tpu as pltpu
from jax.sharding import Mesh, PartitionSpec as P

D = 32
K = 8
DESC = 512
NB = 30
TW = 17 * 128


def kernel(mine_ref, other_ref, refs_ref, left_ref, right_ref, taps_ref, flag_ref, place_ref,
           o_ref, qs, rs, base, res, cmask, sems):
    scale = DESC ** -0.5
    zh, core = place_ref[0], place_ref[1]
    for s in range(4):
        for ref, c in ((mine_ref, core), (other_ref, 1 - core)):
            w = 2 * lax.rem(zh - s + 4, 4) + c
            qs[pl.ds(pl.multiple_of(256 + w * 64, 64), 64), :] = ref[s * 128:s * 128 + 64, :]
            rim = jnp.where(w >= 4, (w - 4) * 64, 768 + w * 64)
            qs[pl.ds(pl.multiple_of(rim, 64), 64), :] = ref[s * 128 + 64:s * 128 + 128, :]
    rs[0:128, :] = jnp.zeros((128, DESC), rs.dtype)
    rs[2112:2304, :] = jnp.zeros((192, DESC), rs.dtype)
    rs[128:384, :] = left_ref[...]
    rs[384:1920, :] = refs_ref[...]
    rs[1920:2112, :] = right_ref[...]
    j = lax.broadcasted_iota(jnp.int32, (8, 128), 1) - 128
    for t in range(17):
        for c in range(4):
            jt = j + (t * 128 + c * D)
            cmask[t, c] = jnp.where(jt < 256, flag_ref[2], jnp.where(jt >= 1792, flag_ref[3], 1.0))

    def scores(c, first, width):
        us = range(c, NB, 4)
        lhs = jnp.concatenate([qs[u * D:(u + 1) * D, :] for u in us], axis=0)
        rhs = rs[pl.ds(pl.multiple_of(first + c * D, D), width), :]
        s = lax.dot_general(lhs, rhs, (((1,), (1,)), ((), ())), preferred_element_type=jnp.float32)
        s = jnp.tanh(s * scale)
        first = first // 128
        for h in range(width // 128):
            for n, u in enumerate(us):
                for v in range(4):
                    base[first + h, v, u] = s[n * D + v * 8:n * D + v * 8 + 8, h * 128:h * 128 + 128]

    for c in range(4):
        def col(t, _, c=c):
            scores(c, t * 256 + (128 if c == 0 else 0), 256)
            return 0

        lax.fori_loop(0, 8, col, 0)
    scores(1, 2048, 128)

    lane = lax.broadcasted_iota(jnp.int32, (8, 128), 1)

    def filters(p):
        w = [taps_ref[p, k] for k in range(K)]
        even, odd = w[0::2], w[1::2]
        return even, odd, [a + b for a, b in zip(even, odd)]

    banks = [filters(0), filters(1)]

    def total(w, vals):
        p = [a * b for a, b in zip(w, vals)]
        return (p[0] + p[1]) + (p[2] + p[3])

    def taps_of(bank, x):
        even, odd, both = bank
        memo = {}

        def once(key, fn):
            if key not in memo:
                memo[key] = fn()
            return memo[key]

        def pair(n):
            return once(("s", n), lambda: x(2 * n) + x(2 * n - 1))

        def a(n):
            return once(("a", n), lambda: total(even, [x(2 * (n + j - 2)) for j in range(4)]))

        def b(n):
            return once(("b", n), lambda: total(odd, [x(2 * (n + j - 2) - 1) for j in range(4)]))

        def y(u):
            if u % 2 == 0:
                return a(u // 2) + b(u // 2 + 1)
            n = (u + 1) // 2
            return total(both, [pair(n + j - 2) for j in range(4)]) - (a(n) + b(n))

        return y

    def chain(m, v, lo, hi, masked):
        a0 = (lo - 8) // 4
        d_view = base.at[pl.ds(m + a0 + 1, (hi + 6) // 4 - a0 + 1), v]
        m_view = cmask.at[pl.ds(m + a0 + 1, (hi + 6) // 4 - a0 + 1)]
        o_view = res.at[pl.ds(m + lo // 4 - 1, (hi - lo) // 4 + 2), pl.ds(pl.multiple_of(v * 8, 8), 488)]
        d, f = {}, {}

        def load(u):
            if u not in d:
                d[u] = d_view[u // 4 - a0, u]
            return d[u]

        y0 = taps_of(banks[0], load)
        y1 = taps_of(banks[1], f.__getitem__)
        for u in range(lo - 4, hi + 4):
            x = jnp.tanh(y0(u))
            if masked:
                x = x * m_view[u // 4 - a0, u % 4]
            if u < 8:
                x = x * flag_ref[0]
            if u >= 24:
                x = x * flag_ref[1]
            f[u] = x
            w = u - 3
            if w >= lo:
                o = jnp.tanh(y1(w))
                c, at, r = w % 4, w // 4 - lo // 4, (w - 8) * D
                if c == 0:
                    o_view[at, r:r + 8] = o
                else:
                    o = pltpu.roll(o, 32 * c, 1)
                    pltpu.store(o_view.at[at, r:r + 8], o, mask=lane >= 32 * c)
                    pltpu.store(o_view.at[at + 1, r:r + 8], o, mask=lane < 32 * c)

    def out_copy(n):
        return pltpu.make_async_copy(
            res.at[n + 1],
            o_ref.at[:, pl.ds(pl.multiple_of(n * 128, 128), 128)], sems.at[n])

    def diagonals(m0, m1, lo, hi, masked, send):
        def step(m, _):
            def part(i, _):
                for n in range(VP):
                    chain(m, i * VP + n, lo, hi, masked)
                return 0

            lax.fori_loop(0, 4 // VP, part, 0)
            if send:
                out_copy(m).start()
            return 0

        lax.fori_loop(m0, m1, step, 0)

    diagonals(-4, -3, 20, 23, True, False)
    diagonals(-3, -2, 16, 23, True, False)
    diagonals(-2, -1, 12, 23, True, False)
    diagonals(-1, 0, 8, 23, True, False)
    diagonals(0, 9, 8, 23, True, True)
    diagonals(9, 10, 8, 19, True, True)
    diagonals(10, 11, 8, 15, True, True)
    diagonals(11, 12, 8, 11, True, True)
    for n in range(12):
        out_copy(n).wait()


VP = 2


def tile(*args):
    vmem, smem = pl.BlockSpec(memory_space=pltpu.VMEM), pl.BlockSpec(memory_space=pltpu.SMEM)
    return pl.pallas_call(
        kernel,
        out_shape=jax.ShapeDtypeStruct((512, 1536), jnp.float32),
        in_specs=[vmem] * 5 + [smem] * 3,
        out_specs=pl.BlockSpec(memory_space=pl.ANY),
        scratch_shapes=[
            pltpu.VMEM((1024, DESC), jnp.bfloat16),
            pltpu.VMEM((2304, DESC), jnp.bfloat16),
            pltpu.VMEM((17, 4, NB, 8, 128), jnp.float32),
            pltpu.VMEM((14, 512, 128), jnp.float32),
            pltpu.VMEM((17, 4, 8, 128), jnp.float32),
            pltpu.SemaphoreType.DMA((12,)),
        ],
        compiler_params=pltpu.CompilerParams(vmem_limit_bytes=40 << 20),
        cost_estimate=pl.CostEstimate(flops=2 * 960 * 1984 * 512, bytes_accessed=6 << 20, transcendentals=0),
    )(*args)


def grid_perm(sizes, move):
    pairs = []
    for src in np.ndindex(*sizes):
        dst = move(*src)
        if dst is not None:
            pairs.append((int(np.ravel_multi_index(src, sizes)), int(np.ravel_multi_index(dst, sizes))))
    return pairs


PB = ("x", "y", "zl")
ROW = ("zh", "c")
SIZES = (4, 4, 2, 4, 2)


def local(q, r, taps):
    pb, row = lax.axis_index(PB), lax.axis_index(ROW)

    def halo_move(x, y, zl, zh, c):
        p, w = (x * 4 + y) * 2 + zl, zh * 2 + c
        p = p + 1 if w >= 4 else p - 1
        if p < 0 or p > 31:
            return None
        return (p // 8, p // 2 % 4, p % 2, zh, c)

    halo = lax.ppermute(q, PB + ROW, grid_perm(SIZES, halo_move))
    both = jnp.concatenate([q, halo], axis=0)
    zh = lax.axis_index("zh")
    shifted = [lax.ppermute(both, "zh", [(i, (i + d) % 4) for i in range(4)]) for d in (1, 2, 3)]
    stack = jnp.concatenate([both] + shifted, axis=0)
    other = lax.ppermute(stack, "c", [(0, 1), (1, 0)])

    refs = lax.all_to_all(jnp.broadcast_to(r[None], (32, 48, DESC)), PB, 0, 0, tiled=True).reshape(1536, DESC)
    left = lax.ppermute(refs[1280:], ROW, [(i, i + 1) for i in range(7)])
    right = lax.ppermute(refs[:192], ROW, [(i + 1, i) for i in range(7)])
    flags = jnp.stack([pb != 0, pb != 31, row != 0, row != 7]).astype(jnp.float32)
    place = jnp.stack([zh, lax.axis_index("c")])
    return tile(stack, other, refs, left, right, taps, flags, place)


def solution(mesh):
    split = Mesh(mesh.devices.reshape(SIZES), PB + ROW)
    specs = (P(PB + ROW, None), P(ROW + PB, None), P())
    return jax.shard_map(local, mesh=split, in_specs=specs, out_specs=P(PB, ROW), check_vma=False)
```

```python
import jax
import jax.numpy as jnp
import numpy as np
from jax import lax
from jax.experimental import pallas as pl
from jax.experimental.pallas import tpu as pltpu
from jax.sharding import Mesh, PartitionSpec as P

D = 32
K = 8
DESC = 512
NB = 30
PB = ("x", "y", "zl")
ROW = ("zh", "c")
SIZES = (4, 4, 2, 4, 2)


def arrange(slot_a, slot_b, slot_c, slot_d, place_ref, refs, send_left, send_right):
    core, second = place_ref[1], place_ref[2]
    inner = jnp.where(core == 0, 384, 96)
    outer = jnp.where(core == 0, 96, 384)
    for s, ref in enumerate((slot_a, slot_b, slot_c, slot_d)):
        at = lax.rem(second - s + 4, 4) * outer
        for i in range(4):
            refs[pl.ds(pl.multiple_of(at + i * inner, 96), 96), :] = ref[i * 96:i * 96 + 96, :]
    send_left[...] = refs[1280:1536, :]
    send_right[...] = refs[0:192, :]


def score_tiles(qs, base, rhs, first, count):
    scale = DESC ** -0.5
    for c in range(4):
        us = range(c, NB, 4)
        lhs = jnp.concatenate([qs[u * D:(u + 1) * D, :] for u in us], axis=0)
        s = lax.dot_general(lhs, rhs(c), (((1,), (1,)), ((), ())), preferred_element_type=jnp.float32)
        s = jnp.tanh(s * scale)
        for h in range(count):
            for n, u in enumerate(us):
                for v in range(4):
                    base[first + h, v, u] = s[n * D + v * 8:n * D + v * 8 + 8, h * 128:h * 128 + 128]


def make_diagonals(base, res, taps_ref, flag_ref, cmask):
    lane = lax.broadcasted_iota(jnp.int32, (8, 128), 1)

    def filters(p):
        w = [taps_ref[p, k] for k in range(K)]
        even, odd = w[0::2], w[1::2]
        return even, odd, [a + b for a, b in zip(even, odd)]


    def total(w, vals):
        p = [a * b for a, b in zip(w, vals)]
        return (p[0] + p[1]) + (p[2] + p[3])

    banks = [filters(0), filters(1)]

    def taps_of(bank, x):
        even, odd, both = bank
        memo = {}

        def once(key, fn):
            if key not in memo:
                memo[key] = fn()
            return memo[key]

        def pair(n):
            return once(("s", n), lambda: x(2 * n) + x(2 * n - 1))

        def a(n):
            return once(("a", n), lambda: total(even, [x(2 * (n + j - 2)) for j in range(4)]))

        def b(n):
            return once(("b", n), lambda: total(odd, [x(2 * (n + j - 2) - 1) for j in range(4)]))

        def y(u):
            if u % 2 == 0:
                return a(u // 2) + b(u // 2 + 1)
            n = (u + 1) // 2
            return total(both, [pair(n + j - 2) for j in range(4)]) - (a(n) + b(n))

        return y

    def chain(m, v, lo, hi, masked):
        a0 = (lo - 8) // 4
        d_view = base.at[pl.ds(m + a0 + 1, (hi + 6) // 4 - a0 + 1), v]
        m_view = cmask.at[pl.ds(m + a0 + 1, (hi + 6) // 4 - a0 + 1)] if masked else None
        o_view = res.at[pl.ds(m + lo // 4 - 1, (hi - lo) // 4 + 2), pl.ds(pl.multiple_of(v * 8, 8), 488)]
        d, f = {}, {}

        def load(u):
            if u not in d:
                d[u] = d_view[u // 4 - a0, u]
            return d[u]

        y0 = taps_of(banks[0], load)
        y1 = taps_of(banks[1], f.__getitem__)
        for u in range(lo - 4, hi + 4):
            x = jnp.tanh(y0(u))
            if masked:
                x = x * m_view[u // 4 - a0, u % 4]
            if u < 8:
                x = x * flag_ref[0]
            if u >= 24:
                x = x * flag_ref[1]
            f[u] = x
            w = u - 3
            if w >= lo:
                o = jnp.tanh(y1(w))
                c, at, r = w % 4, w // 4 - lo // 4, (w - 8) * D
                if c == 0:
                    o_view[at, r:r + 8] = o
                else:
                    o = pltpu.roll(o, 32 * c, 1)
                    pltpu.store(o_view.at[at, r:r + 8], o, mask=lane >= 32 * c)
                    pltpu.store(o_view.at[at + 1, r:r + 8], o, mask=lane < 32 * c)

    def diagonals(m0, m1, lo, hi, masked, after=None):
        def step(m, _):
            for v in range(4):
                chain(m, v, lo, hi, masked)
            if after is not None:
                after(m)
            return 0

        lax.fori_loop(m0, m1, step, 0)

    return diagonals


def middle(mine_ref, other_ref, refs_ref, taps_ref, flag_ref, place_ref, qs, base, res):
    zh, core = place_ref[0], place_ref[1]
    for s in range(4):
        for ref, c in ((mine_ref, core), (other_ref, 1 - core)):
            w = 2 * lax.rem(zh - s + 4, 4) + c
            qs[pl.ds(pl.multiple_of(256 + w * 64, 64), 64), :] = ref[s * 128:s * 128 + 64, :]
            rim = jnp.where(w >= 4, (w - 4) * 64, 768 + w * 64)
            qs[pl.ds(pl.multiple_of(rim, 64), 64), :] = ref[s * 128 + 64:s * 128 + 128, :]

    def rows(start, size):
        return lambda c: refs_ref[pl.ds(pl.multiple_of(start + c * D, D), size), :]

    def pair(i, _):
        score_tiles(qs, base, rows(i * 256, 256), 3 + 2 * i, 2)
        return 0

    lax.fori_loop(0, 5, pair, 0)
    score_tiles(qs, base, rows(1280, 128), 13, 1)
    make_diagonals(base, res, taps_ref, flag_ref, None)(2, 6, 8, 23, False)


def edges(base_in, res_in, qs, refs_ref, left_ref, right_ref, taps_ref, flag_ref,
          base, res, o_ref, lo_rows, hi_rows, cmask, sems):
    lo_rows[0:128, :] = jnp.zeros((128, DESC), lo_rows.dtype)
    lo_rows[128:384, :] = left_ref[...]
    lo_rows[384:512, :] = refs_ref[0:128, :]
    hi_rows[0:128, :] = refs_ref[1408:1536, :]
    hi_rows[128:320, :] = right_ref[...]
    hi_rows[320:512, :] = jnp.zeros((192, DESC), hi_rows.dtype)
    for rows, first in ((lo_rows, 0), (hi_rows, 14)):
        score_tiles(qs, base, lambda c: rows[c * D:c * D + 384, :], first, 3)
    j = lax.broadcasted_iota(jnp.int32, (8, 128), 1) - 128
    for t in range(17):
        for c in range(4):
            jt = j + (t * 128 + c * D)
            cmask[t, c] = jnp.where(jt < 256, flag_ref[2], jnp.where(jt >= 1792, flag_ref[3], 1.0))

    def out_copy(n):
        return pltpu.make_async_copy(
            res.at[n + 1], o_ref.at[:, pl.ds(pl.multiple_of(n * 128, 128), 128)], sems.at[n])

    def send(m):
        out_copy(m).start()

    diagonals = make_diagonals(base, res, taps_ref, flag_ref, cmask)
    diagonals(-4, -3, 20, 23, True)
    diagonals(-3, -2, 16, 23, True)
    diagonals(-2, -1, 12, 23, True)
    diagonals(-1, 0, 8, 23, True)
    diagonals(0, 2, 8, 23, True, send)
    for n in range(2, 6):
        send(n)
    diagonals(6, 9, 8, 23, True, send)
    diagonals(9, 10, 8, 19, True, send)
    diagonals(10, 11, 8, 15, True, send)
    diagonals(11, 12, 8, 11, True, send)
    for n in range(12):
        out_copy(n).wait()


VMEM = pl.BlockSpec(memory_space=pltpu.VMEM)
SMEM = pl.BlockSpec(memory_space=pltpu.SMEM)


def rows_of(n):
    return jax.ShapeDtypeStruct((n, DESC), jnp.bfloat16)


def f32(*shape):
    return jax.ShapeDtypeStruct(shape, jnp.float32)


def params(mib):
    return pltpu.CompilerParams(vmem_limit_bytes=mib << 20)


def cost(flops, size):
    return pl.CostEstimate(flops=flops, bytes_accessed=size, transcendentals=0)


BASE, RES = (17, 4, NB, 8, 128), (14, 512, 128)


def pack(a, b, c, d, stack):
    for s, ref in enumerate((a, b, c, d)):
        stack[s * 128:s * 128 + 128, :] = ref[...]


def run_pack(parts):
    return pl.pallas_call(
        pack, out_shape=rows_of(512), in_specs=[VMEM] * 4, out_specs=VMEM,
        compiler_params=params(4), cost_estimate=cost(0, 1 << 20))(*parts)


def run_arrange(slots, place):
    return pl.pallas_call(
        arrange, out_shape=[rows_of(1536), rows_of(256), rows_of(192)],
        in_specs=[VMEM] * 4 + [SMEM], out_specs=[VMEM] * 3,
        compiler_params=params(8), cost_estimate=cost(0, 3 << 20))(*slots, place)


def run_middle(mine, other, refs, taps, flags, place):
    return pl.pallas_call(
        middle, out_shape=[rows_of(1024), f32(*BASE), f32(*RES)],
        in_specs=[VMEM] * 3 + [SMEM] * 3, out_specs=[VMEM] * 3,
        compiler_params=params(20), cost_estimate=cost(1 << 32, 12 << 20))(mine, other, refs, taps, flags, place)


def run_edges(base, res, qs, refs, left, right, taps, flags):
    return pl.pallas_call(
        edges, out_shape=[f32(*BASE), f32(*RES), f32(512, 1536)],
        in_specs=[VMEM] * 6 + [SMEM] * 2, out_specs=[VMEM] * 2 + [pl.BlockSpec(memory_space=pl.ANY)],
        scratch_shapes=[pltpu.VMEM((512, DESC), jnp.bfloat16), pltpu.VMEM((512, DESC), jnp.bfloat16),
                        pltpu.VMEM((17, 4, 8, 128), jnp.float32), pltpu.SemaphoreType.DMA((12,))],
        input_output_aliases={0: 0, 1: 1},
        compiler_params=params(20), cost_estimate=cost(1 << 32, 12 << 20))(base, res, qs, refs, left, right, taps, flags)[2]


def move_rows(value, move):
    pairs = []
    for src in np.ndindex(*SIZES):
        dst = move(*src)
        if dst is not None:
            pairs.append((int(np.ravel_multi_index(src, SIZES)), int(np.ravel_multi_index(dst, SIZES))))
    return lax.ppermute(value, PB + ROW, pairs)


def rim_of_queries(x, y, zl, zh, c):
    p, w = (x * 4 + y) * 2 + zl, zh * 2 + c
    p = p + 1 if w >= 4 else p - 1
    return None if p < 0 or p > 31 else (p // 8, p // 2 % 4, p % 2, zh, c)


def along_second(d):
    def move(x, y, zl, zh, c):
        return (x, (y + d) % 4, zl, zh, c) if c == 0 else ((x + d) % 4, y, zl, zh, c)

    return move


def first_groups():
    at = lambda *i: int(np.ravel_multi_index(i, (4, 4, 2, 2)))
    rows = [[at(x, y, z, 0) for x in range(4) for z in range(2)] for y in range(4)]
    return rows + [[at(x, y, z, 1) for y in range(4) for z in range(2)] for x in range(4)]


def local(q, r, taps):
    index = {a: lax.axis_index(a) for a in PB + ROW}
    pb, row = lax.axis_index(PB), lax.axis_index(ROW)
    second = jnp.where(index["c"] == 0, index["y"], index["x"])
    flags = jnp.stack([pb != 0, pb != 31, row != 0, row != 7]).astype(jnp.float32)
    place = jnp.stack([index["zh"], index["c"], second])

    rim = move_rows(q, rim_of_queries)
    block = lax.all_to_all(jnp.broadcast_to(r[None], (8, 48, DESC)), PB + ("c",), 0, 0,
                           axis_index_groups=first_groups(), tiled=True).reshape(384, DESC)
    both = jnp.concatenate([q, rim], axis=0)
    turned = [lax.ppermute(both, "zh", [(i, (i + d) % 4) for i in range(4)]) for d in (1, 2, 3)]
    stack = run_pack([both] + turned)
    other = lax.ppermute(stack, "c", [(0, 1), (1, 0)])
    slots = [block] + [move_rows(block, along_second(d)) for d in (1, 2, 3)]
    refs, send_left, send_right = run_arrange(slots, place)
    left = lax.ppermute(send_left, ROW, [(i, i + 1) for i in range(7)])
    right = lax.ppermute(send_right, ROW, [(i + 1, i) for i in range(7)])
    qs, base, res = run_middle(stack, other, refs, taps, flags, place)
    return run_edges(base, res, qs, refs, left, right, taps, flags)


def solution(mesh):
    split = Mesh(mesh.devices.reshape(SIZES), PB + ROW)
    specs = (P(PB + ROW, None), P(ROW + PB, None), P())
    return jax.shard_map(local, mesh=split, in_specs=specs, out_specs=P(PB, ROW), check_vma=False)
```

```python
import jax
import jax.numpy as jnp
import numpy as np
from jax import lax
from jax.experimental import pallas as pl
from jax.experimental.pallas import tpu as pltpu
from jax.sharding import Mesh, PartitionSpec as P

D = 32
K = 8
DESC = 512
NB = 30
PB = ("x", "y", "zl")
ROW = ("zh", "c")
SIZES = (4, 4, 2, 4, 2)


def arrange(slot_a, slot_b, slot_c, slot_d, place_ref, refs, send_left, send_right):
    core, second = place_ref[1], place_ref[2]
    inner = jnp.where(core == 0, 384, 96)
    outer = jnp.where(core == 0, 96, 384)
    for s, ref in enumerate((slot_a, slot_b, slot_c, slot_d)):
        at = lax.rem(second - s + 4, 4) * outer
        for i in range(4):
            refs[pl.ds(pl.multiple_of(at + i * inner, 96), 96), :] = ref[i * 96:i * 96 + 96, :]
    send_left[...] = refs[1280:1536, :]
    send_right[...] = refs[0:192, :]


def score_tiles(qs, base, rhs, first, count):
    scale = DESC ** -0.5
    for c in range(4):
        us = range(c, NB, 4)
        lhs = jnp.concatenate([qs[u * D:(u + 1) * D, :] for u in us], axis=0)
        s = lax.dot_general(lhs, rhs(c), (((1,), (1,)), ((), ())), preferred_element_type=jnp.float32)
        s = jnp.tanh(s * scale)
        for h in range(count):
            for n, u in enumerate(us):
                for v in range(4):
                    base[first + h, v, u] = s[n * D + v * 8:n * D + v * 8 + 8, h * 128:h * 128 + 128]


def make_diagonals(base, res, taps_ref, flag_ref, cmask):
    lane = lax.broadcasted_iota(jnp.int32, (8, 128), 1)

    def filters(p):
        w = [taps_ref[p, k] for k in range(K)]
        even, odd = w[0::2], w[1::2]
        return even, odd, [a + b for a, b in zip(even, odd)]


    def total(w, vals):
        p = [a * b for a, b in zip(w, vals)]
        return (p[0] + p[1]) + (p[2] + p[3])

    banks = [filters(0), filters(1)]

    def taps_of(bank, x):
        even, odd, both = bank
        memo = {}

        def once(key, fn):
            if key not in memo:
                memo[key] = fn()
            return memo[key]

        def pair(n):
            return once(("s", n), lambda: x(2 * n) + x(2 * n - 1))

        def a(n):
            return once(("a", n), lambda: total(even, [x(2 * (n + j - 2)) for j in range(4)]))

        def b(n):
            return once(("b", n), lambda: total(odd, [x(2 * (n + j - 2) - 1) for j in range(4)]))

        def y(u):
            if u % 2 == 0:
                return a(u // 2) + b(u // 2 + 1)
            n = (u + 1) // 2
            return total(both, [pair(n + j - 2) for j in range(4)]) - (a(n) + b(n))

        return y

    def chain(m, v, lo, hi, masked):
        a0 = (lo - 8) // 4
        d_view = base.at[pl.ds(m + a0 + 1, (hi + 6) // 4 - a0 + 1), v]
        m_view = cmask.at[pl.ds(m + a0 + 1, (hi + 6) // 4 - a0 + 1)] if masked else None
        o_view = res.at[pl.ds(m + lo // 4 - 1, (hi - lo) // 4 + 2), pl.ds(pl.multiple_of(v * 8, 8), 488)]
        d, f = {}, {}

        def load(u):
            if u not in d:
                d[u] = d_view[u // 4 - a0, u]
            return d[u]

        y0 = taps_of(banks[0], load)
        y1 = taps_of(banks[1], f.__getitem__)
        for u in range(lo - 4, hi + 4):
            x = jnp.tanh(y0(u))
            if masked:
                x = x * m_view[u // 4 - a0, u % 4]
            if u < 8:
                x = x * flag_ref[0]
            if u >= 24:
                x = x * flag_ref[1]
            f[u] = x
            w = u - 3
            if w >= lo:
                o = jnp.tanh(y1(w))
                c, at, r = w % 4, w // 4 - lo // 4, (w - 8) * D
                if c == 0:
                    o_view[at, r:r + 8] = o
                else:
                    o = pltpu.roll(o, 32 * c, 1)
                    pltpu.store(o_view.at[at, r:r + 8], o, mask=lane >= 32 * c)
                    pltpu.store(o_view.at[at + 1, r:r + 8], o, mask=lane < 32 * c)

    def diagonals(m0, m1, lo, hi, masked, after=None):
        def step(m, _):
            for v in range(4):
                chain(m, v, lo, hi, masked)
            if after is not None:
                after(m)
            return 0

        lax.fori_loop(m0, m1, step, 0)

    return diagonals


def middle(mine_ref, near_ref, far_ref, refs_ref, taps_ref, flag_ref, place_ref, qs, base, res):
    zh, core = place_ref[0], place_ref[1]

    def put(ref, at, z, c):
        w = 2 * lax.rem(z + 8, 4) + c
        qs[pl.ds(pl.multiple_of(256 + w * 64, 64), 64), :] = ref[at:at + 64, :]
        rim = jnp.where(w >= 4, (w - 4) * 64, 768 + w * 64)
        qs[pl.ds(pl.multiple_of(rim, 64), 64), :] = ref[at + 64:at + 128, :]

    put(mine_ref, 0, zh, core)
    put(mine_ref, 128, zh, 1 - core)
    for ref, c in ((near_ref, core), (far_ref, 1 - core)):
        z = zh - 1 + 2 * c
        put(ref, 0, z, c)
        put(ref, 128, z, 1 - c)
        put(ref, 256, zh + 2, c)

    def rows(start, size):
        return lambda c: refs_ref[pl.ds(pl.multiple_of(start + c * D, D), size), :]

    def pair(i, _):
        score_tiles(qs, base, rows(i * 256, 256), 3 + 2 * i, 2)
        return 0

    lax.fori_loop(0, 5, pair, 0)
    score_tiles(qs, base, rows(1280, 128), 13, 1)
    make_diagonals(base, res, taps_ref, flag_ref, None)(2, 6, 8, 23, False)


def edges(base_in, res_in, qs, refs_ref, left_ref, right_ref, taps_ref, flag_ref,
          base, res, o_ref, lo_rows, hi_rows, cmask, sems):
    lo_rows[0:128, :] = jnp.zeros((128, DESC), lo_rows.dtype)
    lo_rows[128:384, :] = left_ref[...]
    lo_rows[384:512, :] = refs_ref[0:128, :]
    hi_rows[0:128, :] = refs_ref[1408:1536, :]
    hi_rows[128:320, :] = right_ref[...]
    hi_rows[320:512, :] = jnp.zeros((192, DESC), hi_rows.dtype)
    for rows, first in ((lo_rows, 0), (hi_rows, 14)):
        score_tiles(qs, base, lambda c: rows[c * D:c * D + 384, :], first, 3)
    j = lax.broadcasted_iota(jnp.int32, (8, 128), 1) - 128
    for t in range(17):
        for c in range(4):
            jt = j + (t * 128 + c * D)
            cmask[t, c] = jnp.where(jt < 256, flag_ref[2], jnp.where(jt >= 1792, flag_ref[3], 1.0))

    def out_copy(n):
        return pltpu.make_async_copy(
            res.at[n + 1], o_ref.at[:, pl.ds(pl.multiple_of(n * 128, 128), 128)], sems.at[n])

    def send(m):
        out_copy(m).start()

    diagonals = make_diagonals(base, res, taps_ref, flag_ref, cmask)
    diagonals(-4, -3, 20, 23, True)
    diagonals(-3, -2, 16, 23, True)
    diagonals(-2, -1, 12, 23, True)
    diagonals(-1, 0, 8, 23, True)
    diagonals(0, 2, 8, 23, True, send)
    for n in range(2, 6):
        send(n)
    diagonals(6, 9, 8, 23, True, send)
    diagonals(9, 10, 8, 19, True, send)
    diagonals(10, 11, 8, 15, True, send)
    diagonals(11, 12, 8, 11, True, send)
    for n in range(12):
        out_copy(n).wait()


VMEM = pl.BlockSpec(memory_space=pltpu.VMEM)
SMEM = pl.BlockSpec(memory_space=pltpu.SMEM)


def rows_of(n):
    return jax.ShapeDtypeStruct((n, DESC), jnp.bfloat16)


def f32(*shape):
    return jax.ShapeDtypeStruct(shape, jnp.float32)


def params(mib):
    return pltpu.CompilerParams(vmem_limit_bytes=mib << 20)


def cost(flops, size):
    return pl.CostEstimate(flops=flops, bytes_accessed=size, transcendentals=0)


BASE, RES = (17, 4, NB, 8, 128), (14, 512, 128)


def pack(*refs):
    at = 0
    for ref in refs[:-1]:
        refs[-1][at:at + ref.shape[0], :] = ref[...]
        at += ref.shape[0]


def run_pack(*parts):
    return pl.pallas_call(
        pack, out_shape=rows_of(sum(p.shape[0] for p in parts)), in_specs=[VMEM] * len(parts), out_specs=VMEM,
        compiler_params=params(4), cost_estimate=cost(0, 1 << 20))(*parts)


def head(ref, out):
    out[...] = ref[0:128, :]


def run_head(value):
    return pl.pallas_call(
        head, out_shape=rows_of(128), in_specs=[VMEM], out_specs=VMEM,
        compiler_params=params(4), cost_estimate=cost(0, 1 << 18))(value)


def run_arrange(slots, place):
    return pl.pallas_call(
        arrange, out_shape=[rows_of(1536), rows_of(256), rows_of(192)],
        in_specs=[VMEM] * 4 + [SMEM], out_specs=[VMEM] * 3,
        compiler_params=params(8), cost_estimate=cost(0, 3 << 20))(*slots, place)


def run_middle(mine, near, far, refs, taps, flags, place):
    return pl.pallas_call(
        middle, out_shape=[rows_of(1024), f32(*BASE), f32(*RES)],
        in_specs=[VMEM] * 4 + [SMEM] * 3, out_specs=[VMEM] * 3,
        compiler_params=params(20), cost_estimate=cost(1 << 32, 12 << 20))(mine, near, far, refs, taps, flags, place)


def run_edges(base, res, qs, refs, left, right, taps, flags):
    return pl.pallas_call(
        edges, out_shape=[f32(*BASE), f32(*RES), f32(512, 1536)],
        in_specs=[VMEM] * 6 + [SMEM] * 2, out_specs=[VMEM] * 2 + [pl.BlockSpec(memory_space=pl.ANY)],
        scratch_shapes=[pltpu.VMEM((512, DESC), jnp.bfloat16), pltpu.VMEM((512, DESC), jnp.bfloat16),
                        pltpu.VMEM((17, 4, 8, 128), jnp.float32), pltpu.SemaphoreType.DMA((12,))],
        input_output_aliases={0: 0, 1: 1},
        compiler_params=params(20), cost_estimate=cost(1 << 32, 12 << 20))(base, res, qs, refs, left, right, taps, flags)[2]


def move_rows(value, move):
    pairs = []
    for src in np.ndindex(*SIZES):
        dst = move(*src)
        if dst is not None:
            pairs.append((int(np.ravel_multi_index(src, SIZES)), int(np.ravel_multi_index(dst, SIZES))))
    return lax.ppermute(value, PB + ROW, pairs)


def rim_of_queries(x, y, zl, zh, c):
    p, w = (x * 4 + y) * 2 + zl, zh * 2 + c
    p = p + 1 if w >= 4 else p - 1
    return None if p < 0 or p > 31 else (p // 8, p // 2 % 4, p % 2, zh, c)


def along_second(d):
    def move(x, y, zl, zh, c):
        return (x, (y + d) % 4, zl, zh, c) if c == 0 else ((x + d) % 4, y, zl, zh, c)

    return move


def turn(x, y, zl, zh, c):
    return (x, y, zl, (zh + 1 - 2 * c) % 4, c)


def first_groups():
    at = lambda *i: int(np.ravel_multi_index(i, (4, 4, 2, 2)))
    rows = [[at(x, y, z, 0) for x in range(4) for z in range(2)] for y in range(4)]
    return rows + [[at(x, y, z, 1) for y in range(4) for z in range(2)] for x in range(4)]


def local(q, r, taps):
    index = {a: lax.axis_index(a) for a in PB + ROW}
    pb, row = lax.axis_index(PB), lax.axis_index(ROW)
    second = jnp.where(index["c"] == 0, index["y"], index["x"])
    flags = jnp.stack([pb != 0, pb != 31, row != 0, row != 7]).astype(jnp.float32)
    place = jnp.stack([index["zh"], index["c"], second])

    block = lax.all_to_all(jnp.broadcast_to(r[None], (8, 48, DESC)), PB + ("c",), 0, 0,
                           axis_index_groups=first_groups(), tiled=True).reshape(384, DESC)
    rim = move_rows(q, rim_of_queries)
    both = run_pack(q, rim)
    mine = run_pack(both, lax.ppermute(both, "c", [(0, 1), (1, 0)]))
    near = move_rows(mine, turn)
    part = run_head(near)
    far = move_rows(part, turn)
    near = run_pack(near, far)
    far = lax.ppermute(near, "c", [(0, 1), (1, 0)])
    slots = [block] + [move_rows(block, along_second(d)) for d in (1, 2, 3)]
    refs, send_left, send_right = run_arrange(slots, place)
    left = lax.ppermute(send_left, ROW, [(i, i + 1) for i in range(7)])
    right = lax.ppermute(send_right, ROW, [(i + 1, i) for i in range(7)])
    qs, base, res = run_middle(mine, near, far, refs, taps, flags, place)
    return run_edges(base, res, qs, refs, left, right, taps, flags)


def solution(mesh):
    split = Mesh(mesh.devices.reshape(SIZES), PB + ROW)
    specs = (P(PB + ROW, None), P(ROW + PB, None), P())
    return jax.shard_map(local, mesh=split, in_specs=specs, out_specs=P(PB, ROW), check_vma=False)
```

```python
import jax
import jax.numpy as jnp
import numpy as np
from jax import lax
from jax.experimental import pallas as pl
from jax.experimental.pallas import tpu as pltpu
from jax.sharding import Mesh, PartitionSpec as P

D = 32
K = 8
DESC = 512
NB = 30
PB = ("x", "y", "zl")
ROW = ("zh", "c")
SIZES = (4, 4, 2, 4, 2)


def arrange(slot_a, slot_b, slot_c, slot_d, place_ref, refs, send_left, send_right):
    core, second = place_ref[1], place_ref[2]
    inner = jnp.where(core == 0, 384, 96)
    outer = jnp.where(core == 0, 96, 384)
    for s, ref in enumerate((slot_a, slot_b, slot_c, slot_d)):
        at = lax.rem(second - s + 4, 4) * outer
        for i in range(4):
            refs[pl.ds(pl.multiple_of(at + i * inner, 96), 96), :] = ref[i * 96:i * 96 + 96, :]
    send_left[...] = refs[1280:1536, :]
    send_right[...] = refs[0:192, :]


def score_tiles(qs, base, rhs, first, count):
    scale = DESC ** -0.5
    for c in range(4):
        us = range(c, NB, 4)
        lhs = jnp.concatenate([qs[u * D:(u + 1) * D, :] for u in us], axis=0)
        s = lax.dot_general(lhs, rhs(c), (((1,), (1,)), ((), ())), preferred_element_type=jnp.float32)
        s = jnp.tanh(s * scale)
        for h in range(count):
            for n, u in enumerate(us):
                for v in range(4):
                    base[first + h, v, u] = s[n * D + v * 8:n * D + v * 8 + 8, h * 128:h * 128 + 128]


def make_diagonals(base, res, taps_ref, flag_ref, cmask):
    lane = lax.broadcasted_iota(jnp.int32, (8, 128), 1)

    def filters(p):
        w = [taps_ref[p, k] for k in range(K)]
        even, odd = w[0::2], w[1::2]
        return even, odd, [a + b for a, b in zip(even, odd)]


    def total(w, vals):
        p = [a * b for a, b in zip(w, vals)]
        return (p[0] + p[1]) + (p[2] + p[3])

    banks = [filters(0), filters(1)]

    def taps_of(bank, x):
        even, odd, both = bank
        memo = {}

        def once(key, fn):
            if key not in memo:
                memo[key] = fn()
            return memo[key]

        def pair(n):
            return once(("s", n), lambda: x(2 * n) + x(2 * n - 1))

        def a(n):
            return once(("a", n), lambda: total(even, [x(2 * (n + j - 2)) for j in range(4)]))

        def b(n):
            return once(("b", n), lambda: total(odd, [x(2 * (n + j - 2) - 1) for j in range(4)]))

        def y(u):
            if u % 2 == 0:
                return a(u // 2) + b(u // 2 + 1)
            n = (u + 1) // 2
            return total(both, [pair(n + j - 2) for j in range(4)]) - (a(n) + b(n))

        return y

    def chain(m, v, lo, hi, masked):
        a0 = (lo - 8) // 4
        d_view = base.at[pl.ds(m + a0 + 1, (hi + 6) // 4 - a0 + 1), v]
        m_view = cmask.at[pl.ds(m + a0 + 1, (hi + 6) // 4 - a0 + 1)] if masked else None
        o_view = res.at[pl.ds(m + lo // 4 - 1, (hi - lo) // 4 + 2), pl.ds(pl.multiple_of(v * 8, 8), 488)]
        d, f = {}, {}

        def load(u):
            if u not in d:
                d[u] = d_view[u // 4 - a0, u]
            return d[u]

        y0 = taps_of(banks[0], load)
        y1 = taps_of(banks[1], f.__getitem__)
        for u in range(lo - 4, hi + 4):
            x = jnp.tanh(y0(u))
            if masked:
                x = x * m_view[u // 4 - a0, u % 4]
            if u < 8:
                x = x * flag_ref[0]
            if u >= 24:
                x = x * flag_ref[1]
            f[u] = x
            w = u - 3
            if w >= lo:
                o = jnp.tanh(y1(w))
                c, at, r = w % 4, w // 4 - lo // 4, (w - 8) * D
                if c == 0:
                    o_view[at, r:r + 8] = o
                else:
                    o = pltpu.roll(o, 32 * c, 1)
                    pltpu.store(o_view.at[at, r:r + 8], o, mask=lane >= 32 * c)
                    pltpu.store(o_view.at[at + 1, r:r + 8], o, mask=lane < 32 * c)

    def diagonals(m0, m1, lo, hi, masked, after=None):
        def step(m, _):
            for v in range(4):
                chain(m, v, lo, hi, masked)
            if after is not None:
                after(m)
            return 0

        lax.fori_loop(m0, m1, step, 0)

    return diagonals


def middle(both_ref, other_ref, near_ref, far_ref, refs_ref, taps_ref, flag_ref, place_ref, qs, base, res):
    zh, core = place_ref[0], place_ref[1]

    def put(ref, at, z, c):
        w = 2 * lax.rem(z + 8, 4) + c
        qs[pl.ds(pl.multiple_of(256 + w * 64, 64), 64), :] = ref[at:at + 64, :]
        rim = jnp.where(w >= 4, (w - 4) * 64, 768 + w * 64)
        qs[pl.ds(pl.multiple_of(rim, 64), 64), :] = ref[at + 64:at + 128, :]

    put(both_ref, 0, zh, core)
    put(other_ref, 0, zh, 1 - core)
    for ref, c in ((near_ref, core), (far_ref, 1 - core)):
        z = zh - 1 + 2 * c
        put(ref, 0, z, c)
        put(ref, 128, z, 1 - c)
        put(ref, 256, zh + 2, c)

    def rows(start, size):
        return lambda c: refs_ref[pl.ds(pl.multiple_of(start + c * D, D), size), :]

    def pair(i, _):
        score_tiles(qs, base, rows(i * 256, 256), 3 + 2 * i, 2)
        return 0

    lax.fori_loop(0, 5, pair, 0)
    score_tiles(qs, base, rows(1280, 128), 13, 1)
    make_diagonals(base, res, taps_ref, flag_ref, None)(2, 6, 8, 23, False)


def edges(base_in, res_in, qs, refs_ref, left_ref, right_ref, taps_ref, flag_ref,
          base, res, o_ref, lo_rows, hi_rows, cmask, sems):
    lo_rows[0:128, :] = jnp.zeros((128, DESC), lo_rows.dtype)
    lo_rows[128:384, :] = left_ref[...]
    lo_rows[384:512, :] = refs_ref[0:128, :]
    hi_rows[0:128, :] = refs_ref[1408:1536, :]
    hi_rows[128:320, :] = right_ref[...]
    hi_rows[320:512, :] = jnp.zeros((192, DESC), hi_rows.dtype)
    for rows, first in ((lo_rows, 0), (hi_rows, 14)):
        score_tiles(qs, base, lambda c: rows[c * D:c * D + 384, :], first, 3)
    j = lax.broadcasted_iota(jnp.int32, (8, 128), 1) - 128
    for t in range(17):
        for c in range(4):
            jt = j + (t * 128 + c * D)
            cmask[t, c] = jnp.where(jt < 256, flag_ref[2], jnp.where(jt >= 1792, flag_ref[3], 1.0))

    def out_copy(n):
        return pltpu.make_async_copy(
            res.at[n + 1], o_ref.at[:, pl.ds(pl.multiple_of(n * 128, 128), 128)], sems.at[n])

    def send(m):
        out_copy(m).start()

    diagonals = make_diagonals(base, res, taps_ref, flag_ref, cmask)
    diagonals(-4, -3, 20, 23, True)
    diagonals(-3, -2, 16, 23, True)
    diagonals(-2, -1, 12, 23, True)
    diagonals(-1, 0, 8, 23, True)
    diagonals(0, 2, 8, 23, True, send)
    for n in range(2, 6):
        send(n)
    diagonals(6, 9, 8, 23, True, send)
    diagonals(9, 10, 8, 19, True, send)
    diagonals(10, 11, 8, 15, True, send)
    diagonals(11, 12, 8, 11, True, send)
    for n in range(12):
        out_copy(n).wait()


VMEM = pl.BlockSpec(memory_space=pltpu.VMEM)
SMEM = pl.BlockSpec(memory_space=pltpu.SMEM)


def rows_of(n):
    return jax.ShapeDtypeStruct((n, DESC), jnp.bfloat16)


def f32(*shape):
    return jax.ShapeDtypeStruct(shape, jnp.float32)


def params(mib):
    return pltpu.CompilerParams(vmem_limit_bytes=mib << 20)


def cost(flops, size):
    return pl.CostEstimate(flops=flops, bytes_accessed=size, transcendentals=0)


BASE, RES = (17, 4, NB, 8, 128), (14, 512, 128)


def pack(*refs):
    at = 0
    for ref in refs[:-1]:
        refs[-1][at:at + ref.shape[0], :] = ref[...]
        at += ref.shape[0]


def run_pack(*parts):
    return pl.pallas_call(
        pack, out_shape=rows_of(sum(p.shape[0] for p in parts)), in_specs=[VMEM] * len(parts), out_specs=VMEM,
        compiler_params=params(4), cost_estimate=cost(0, 1 << 20))(*parts)


def run_arrange(slots, place):
    return pl.pallas_call(
        arrange, out_shape=[rows_of(1536), rows_of(256), rows_of(192)],
        in_specs=[VMEM] * 4 + [SMEM], out_specs=[VMEM] * 3,
        compiler_params=params(8), cost_estimate=cost(0, 3 << 20))(*slots, place)


def run_middle(both, other, near, far, refs, taps, flags, place):
    return pl.pallas_call(
        middle, out_shape=[rows_of(1024), f32(*BASE), f32(*RES)],
        in_specs=[VMEM] * 5 + [SMEM] * 3, out_specs=[VMEM] * 3,
        compiler_params=params(20), cost_estimate=cost(1 << 32, 12 << 20))(both, other, near, far, refs, taps, flags, place)


def run_edges(base, res, qs, refs, left, right, taps, flags):
    return pl.pallas_call(
        edges, out_shape=[f32(*BASE), f32(*RES), f32(512, 1536)],
        in_specs=[VMEM] * 6 + [SMEM] * 2, out_specs=[VMEM] * 2 + [pl.BlockSpec(memory_space=pl.ANY)],
        scratch_shapes=[pltpu.VMEM((512, DESC), jnp.bfloat16), pltpu.VMEM((512, DESC), jnp.bfloat16),
                        pltpu.VMEM((17, 4, 8, 128), jnp.float32), pltpu.SemaphoreType.DMA((12,))],
        input_output_aliases={0: 0, 1: 1},
        compiler_params=params(20), cost_estimate=cost(1 << 32, 12 << 20))(base, res, qs, refs, left, right, taps, flags)[2]


def move_rows(value, move):
    pairs = []
    for src in np.ndindex(*SIZES):
        dst = move(*src)
        if dst is not None:
            pairs.append((int(np.ravel_multi_index(src, SIZES)), int(np.ravel_multi_index(dst, SIZES))))
    return lax.ppermute(value, PB + ROW, pairs)


def rim_of_queries(x, y, zl, zh, c):
    p, w = (x * 4 + y) * 2 + zl, zh * 2 + c
    p = p + 1 if w >= 4 else p - 1
    return None if p < 0 or p > 31 else (p // 8, p // 2 % 4, p % 2, zh, c)


def along_second(d):
    def move(x, y, zl, zh, c):
        return (x, (y + d) % 4, zl, zh, c) if c == 0 else ((x + d) % 4, y, zl, zh, c)

    return move


def turn(x, y, zl, zh, c):
    return (x, y, zl, (zh + 1 - 2 * c) % 4, c)


def first_groups():
    at = lambda *i: int(np.ravel_multi_index(i, (4, 4, 2, 2)))
    rows = [[at(x, y, z, 0) for x in range(4) for z in range(2)] for y in range(4)]
    return rows + [[at(x, y, z, 1) for y in range(4) for z in range(2)] for x in range(4)]


def local(q, r, taps):
    index = {a: lax.axis_index(a) for a in PB + ROW}
    pb, row = lax.axis_index(PB), lax.axis_index(ROW)
    second = jnp.where(index["c"] == 0, index["y"], index["x"])
    flags = jnp.stack([pb != 0, pb != 31, row != 0, row != 7]).astype(jnp.float32)
    place = jnp.stack([index["zh"], index["c"], second])

    rim = move_rows(q, rim_of_queries)
    block = lax.all_to_all(jnp.broadcast_to(r[None], (8, 48, DESC)), PB + ("c",), 0, 0,
                           axis_index_groups=first_groups(), tiled=True).reshape(384, DESC)
    both = run_pack(q, rim)
    near = move_rows(both, turn)
    other = lax.ppermute(both, "c", [(0, 1), (1, 0)])
    rest = move_rows(other, turn)
    far = move_rows(near, turn)
    near = run_pack(near, rest, far)
    far = lax.ppermute(near, "c", [(0, 1), (1, 0)])
    slots = [block] + [move_rows(block, along_second(d)) for d in (1, 2, 3)]
    refs, send_left, send_right = run_arrange(slots, place)
    left = lax.ppermute(send_left, ROW, [(i, i + 1) for i in range(7)])
    right = lax.ppermute(send_right, ROW, [(i + 1, i) for i in range(7)])
    qs, base, res = run_middle(both, other, near, far, refs, taps, flags, place)
    return run_edges(base, res, qs, refs, left, right, taps, flags)


def solution(mesh):
    split = Mesh(mesh.devices.reshape(SIZES), PB + ROW)
    specs = (P(PB + ROW, None), P(ROW + PB, None), P())
    return jax.shard_map(local, mesh=split, in_specs=specs, out_specs=P(PB, ROW), check_vma=False)
```

```python
import jax
import jax.numpy as jnp
import numpy as np
from jax import lax
from jax.experimental import pallas as pl
from jax.experimental.pallas import tpu as pltpu
from jax.sharding import Mesh, PartitionSpec as P

D = 32
K = 8
DESC = 512
NB = 30
PB = ("x", "y", "zl")
ROW = ("zh", "c")
SIZES = (4, 4, 2, 4, 2)


def arrange(slot_a, slot_b, slot_c, slot_d, place_ref, refs, send_far, send_near):
    core, second = place_ref[1], place_ref[2]
    inner = jnp.where(core == 0, 384, 96)
    outer = jnp.where(core == 0, 96, 384)
    for s, ref in enumerate((slot_a, slot_b, slot_c, slot_d)):
        at = lax.rem(second - s + 4, 4) * outer
        for i in range(4):
            refs[pl.ds(pl.multiple_of(at + i * inner, 96), 96), :] = ref[i * 96:i * 96 + 96, :]
    send_far[...] = refs[pl.ds(pl.multiple_of(core * 1280, 256), 256), :]
    send_near[...] = refs[pl.ds(pl.multiple_of((1 - core) * 1280, 256), 256), :]


def score_class(qs, base, rhs, first, count, c):
    us = range(c, NB, 4)
    lhs = jnp.concatenate([qs[u * D:(u + 1) * D, :] for u in us], axis=0)
    s = lax.dot_general(lhs, rhs(c), (((1,), (1,)), ((), ())), preferred_element_type=jnp.float32)
    s = jnp.tanh(s * DESC ** -0.5)
    for h in range(count):
        for n, u in enumerate(us):
            for v in range(4):
                base[first + h, v, u] = s[n * D + v * 8:n * D + v * 8 + 8, h * 128:h * 128 + 128]


def score_tiles(qs, base, rhs, first, count):
    for c in range(4):
        score_class(qs, base, rhs, first, count, c)


def make_diagonals(base, res, taps_ref, flag_ref, cmask):
    lane = lax.broadcasted_iota(jnp.int32, (8, 128), 1)

    def filters(p):
        w = [taps_ref[p, k] for k in range(K)]
        even, odd = w[0::2], w[1::2]
        return even, odd, [a + b for a, b in zip(even, odd)]


    def total(w, vals):
        p = [a * b for a, b in zip(w, vals)]
        return (p[0] + p[1]) + (p[2] + p[3])

    banks = [filters(0), filters(1)]

    def taps_of(bank, x):
        even, odd, both = bank
        memo = {}

        def once(key, fn):
            if key not in memo:
                memo[key] = fn()
            return memo[key]

        def pair(n):
            return once(("s", n), lambda: x(2 * n) + x(2 * n - 1))

        def a(n):
            return once(("a", n), lambda: total(even, [x(2 * (n + j - 2)) for j in range(4)]))

        def b(n):
            return once(("b", n), lambda: total(odd, [x(2 * (n + j - 2) - 1) for j in range(4)]))

        def y(u):
            if u % 2 == 0:
                return a(u // 2) + b(u // 2 + 1)
            n = (u + 1) // 2
            return total(both, [pair(n + j - 2) for j in range(4)]) - (a(n) + b(n))

        return y

    def chain(m, v, lo, hi, masked):
        a0 = (lo - 8) // 4
        d_view = base.at[pl.ds(m + a0 + 1, (hi + 6) // 4 - a0 + 1), v]
        m_view = cmask.at[pl.ds(m + a0 + 1, (hi + 6) // 4 - a0 + 1)] if masked else None
        o_view = res.at[pl.ds(m + lo // 4 - 1, (hi - lo) // 4 + 2), pl.ds(pl.multiple_of(v * 8, 8), 488)]
        d, f = {}, {}

        def load(u):
            if u not in d:
                d[u] = d_view[u // 4 - a0, u]
            return d[u]

        y0 = taps_of(banks[0], load)
        y1 = taps_of(banks[1], f.__getitem__)
        for u in range(lo - 4, hi + 4):
            x = jnp.tanh(y0(u))
            if masked:
                x = x * m_view[u // 4 - a0, u % 4]
            if u < 8:
                x = x * flag_ref[0]
            if u >= 24:
                x = x * flag_ref[1]
            f[u] = x
            w = u - 3
            if w >= lo:
                o = jnp.tanh(y1(w))
                c, at, r = w % 4, w // 4 - lo // 4, (w - 8) * D
                if c == 0:
                    o_view[at, r:r + 8] = o
                else:
                    o = pltpu.roll(o, 32 * c, 1)
                    pltpu.store(o_view.at[at, r:r + 8], o, mask=lane >= 32 * c)
                    pltpu.store(o_view.at[at + 1, r:r + 8], o, mask=lane < 32 * c)

    def diagonals(m0, m1, lo, hi, masked, after=None):
        def step(m, _):
            for v in range(4):
                chain(m, v, lo, hi, masked)
            if after is not None:
                after(m)
            return 0

        lax.fori_loop(m0, m1, step, 0)

    return diagonals, chain


def middle(mine_ref, near_ref, far_ref, refs_ref, taps_ref, flag_ref, place_ref, qs, base, res):
    zh, core = place_ref[0], place_ref[1]

    def put(ref, at, z, c):
        w = 2 * lax.rem(z + 8, 4) + c
        qs[pl.ds(pl.multiple_of(256 + w * 64, 64), 64), :] = ref[at:at + 64, :]
        rim = jnp.where(w >= 4, (w - 4) * 64, 768 + w * 64)
        qs[pl.ds(pl.multiple_of(rim, 64), 64), :] = ref[at + 64:at + 128, :]

    put(mine_ref, 0, zh, core)
    put(mine_ref, 128, zh, 1 - core)
    for ref, c in ((near_ref, core), (far_ref, 1 - core)):
        z = zh - 1 + 2 * c
        put(ref, 0, z, c)
        put(ref, 128, z, 1 - c)
        put(ref, 256, zh + 2, c)

    def rows(start, size):
        return lambda c: refs_ref[pl.ds(pl.multiple_of(start + c * D, D), size), :]

    def pair(i, _):
        score_tiles(qs, base, rows(i * 256, 256), 3 + 2 * i, 2)
        return 0

    lax.fori_loop(0, 4, pair, 0)
    diagonals, chain = make_diagonals(base, res, taps_ref, flag_ref, None)
    for v in range(4):
        score_class(qs, base, rows(1024, 384), 11, 3, v)
        chain(2, v, 8, 23, False)
    diagonals(3, 6, 8, 23, False)
    diagonals(1, 2, 12, 23, False)
    diagonals(6, 7, 8, 19, False)


def edges(base_in, res_in, qs, refs_ref, far_ref, near_ref, taps_ref, flag_ref, place_ref,
          base, res, o_ref, lo_rows, hi_rows, cmask, sems):
    lo_rows[0:128, :] = jnp.zeros((128, DESC), lo_rows.dtype)
    low = place_ref[1] == 0
    lo_rows[128:384, :] = jnp.where(low, far_ref[...], near_ref[...])
    lo_rows[384:512, :] = refs_ref[0:128, :]
    hi_rows[0:128, :] = refs_ref[1408:1536, :]
    hi_rows[128:320, :] = jnp.where(low, near_ref[0:192, :], far_ref[0:192, :])
    hi_rows[320:512, :] = jnp.zeros((192, DESC), hi_rows.dtype)

    def rows(ref):
        return lambda c: ref[c * D:c * D + 384, :]

    score_tiles(qs, base, rows(lo_rows), 0, 3)
    j = lax.broadcasted_iota(jnp.int32, (8, 128), 1) - 128
    for t in range(17):
        for c in range(4):
            jt = j + (t * 128 + c * D)
            cmask[t, c] = jnp.where(jt < 256, flag_ref[2], jnp.where(jt >= 1792, flag_ref[3], 1.0))

    def out_copy(n):
        return pltpu.make_async_copy(
            res.at[n + 1], o_ref.at[:, pl.ds(pl.multiple_of(n * 128, 128), 128)], sems.at[n])

    def send(m):
        out_copy(m).start()

    diagonals, chain = make_diagonals(base, res, taps_ref, flag_ref, cmask)
    for v in range(4):
        score_class(qs, base, rows(hi_rows), 14, 3, v)
        for m in (-4, -3, -2):
            chain(m, v, 4 - 4 * m, 23, True)
    diagonals(-1, 0, 8, 23, True)
    diagonals(0, 1, 8, 23, True, send)
    diagonals(1, 2, 8, 11, True, send)
    for n in range(2, 6):
        send(n)
    diagonals(6, 7, 20, 23, True, send)
    diagonals(7, 9, 8, 23, True, send)
    diagonals(9, 10, 8, 19, True, send)
    diagonals(10, 11, 8, 15, True, send)
    diagonals(11, 12, 8, 11, True, send)
    for n in range(12):
        out_copy(n).wait()


VMEM = pl.BlockSpec(memory_space=pltpu.VMEM)
SMEM = pl.BlockSpec(memory_space=pltpu.SMEM)


def rows_of(n):
    return jax.ShapeDtypeStruct((n, DESC), jnp.bfloat16)


def f32(*shape):
    return jax.ShapeDtypeStruct(shape, jnp.float32)


def params(mib):
    return pltpu.CompilerParams(vmem_limit_bytes=mib << 20)


def cost(flops, size):
    return pl.CostEstimate(flops=flops, bytes_accessed=size, transcendentals=0)


BASE, RES = (17, 4, NB, 8, 128), (14, 512, 128)


def pack(*refs):
    at = 0
    for ref in refs[:-1]:
        refs[-1][at:at + ref.shape[0], :] = ref[...]
        at += ref.shape[0]


def run_pack(*parts):
    return pl.pallas_call(
        pack, out_shape=rows_of(sum(p.shape[0] for p in parts)), in_specs=[VMEM] * len(parts), out_specs=VMEM,
        compiler_params=params(4), cost_estimate=cost(0, 1 << 20))(*parts)


def head(ref, out):
    out[...] = ref[0:128, :]


def run_head(value):
    return pl.pallas_call(
        head, out_shape=rows_of(128), in_specs=[VMEM], out_specs=VMEM,
        compiler_params=params(4), cost_estimate=cost(0, 1 << 18))(value)


def run_arrange(slots, place):
    return pl.pallas_call(
        arrange, out_shape=[rows_of(1536), rows_of(256), rows_of(256)],
        in_specs=[VMEM] * 4 + [SMEM], out_specs=[VMEM] * 3,
        compiler_params=params(8), cost_estimate=cost(0, 3 << 20))(*slots, place)


def run_middle(mine, near, far, refs, taps, flags, place):
    return pl.pallas_call(
        middle, out_shape=[rows_of(1024), f32(*BASE), f32(*RES)],
        in_specs=[VMEM] * 4 + [SMEM] * 3, out_specs=[VMEM] * 3,
        compiler_params=params(20), cost_estimate=cost(1 << 32, 12 << 20))(mine, near, far, refs, taps, flags, place)


def run_edges(base, res, qs, refs, far, near, taps, flags, place):
    return pl.pallas_call(
        edges, out_shape=[f32(*BASE), f32(*RES), f32(512, 1536)],
        in_specs=[VMEM] * 6 + [SMEM] * 3, out_specs=[VMEM] * 2 + [pl.BlockSpec(memory_space=pl.ANY)],
        scratch_shapes=[pltpu.VMEM((512, DESC), jnp.bfloat16), pltpu.VMEM((512, DESC), jnp.bfloat16),
                        pltpu.VMEM((17, 4, 8, 128), jnp.float32), pltpu.SemaphoreType.DMA((12,))],
        input_output_aliases={0: 0, 1: 1},
        compiler_params=params(20), cost_estimate=cost(1 << 32, 12 << 20))(base, res, qs, refs, far, near, taps, flags, place)[2]


def move_rows(value, move):
    pairs = []
    for src in np.ndindex(*SIZES):
        dst = move(*src)
        if dst is not None:
            pairs.append((int(np.ravel_multi_index(src, SIZES)), int(np.ravel_multi_index(dst, SIZES))))
    return lax.ppermute(value, PB + ROW, pairs)


def rim_of_queries(x, y, zl, zh, c):
    p, w = (x * 4 + y) * 2 + zl, zh * 2 + c
    p = p + 1 if w >= 4 else p - 1
    return None if p < 0 or p > 31 else (p // 8, p // 2 % 4, p % 2, zh, c)


def along_second(d):
    def move(x, y, zl, zh, c):
        return (x, (y + d) % 4, zl, zh, c) if c == 0 else ((x + d) % 4, y, zl, zh, c)

    return move


def turn(x, y, zl, zh, c):
    return (x, y, zl, (zh + 1 - 2 * c) % 4, c)


def across(x, y, zl, zh, c):
    z = zh - 1 + 2 * c
    return None if z < 0 or z > 3 else (x, y, zl, z, 1 - c)


def first_groups():
    at = lambda *i: int(np.ravel_multi_index(i, (4, 4, 2, 2)))
    rows = [[at(x, y, z, 0) for x in range(4) for z in range(2)] for y in range(4)]
    return rows + [[at(x, y, z, 1) for y in range(4) for z in range(2)] for x in range(4)]


def local(q, r, taps):
    index = {a: lax.axis_index(a) for a in PB + ROW}
    pb, row = lax.axis_index(PB), lax.axis_index(ROW)
    second = jnp.where(index["c"] == 0, index["y"], index["x"])
    flags = jnp.stack([pb != 0, pb != 31, row != 0, row != 7]).astype(jnp.float32)
    place = jnp.stack([index["zh"], index["c"], second])

    block = lax.all_to_all(jnp.broadcast_to(r[None], (8, 48, DESC)), PB + ("c",), 0, 0,
                           axis_index_groups=first_groups(), tiled=True).reshape(384, DESC)
    rim = move_rows(q, rim_of_queries)
    both = run_pack(q, rim)
    mine = run_pack(both, lax.ppermute(both, "c", [(0, 1), (1, 0)]))
    near = move_rows(mine, turn)
    part = run_head(near)
    far = move_rows(part, turn)
    near = run_pack(near, far)
    far = lax.ppermute(near, "c", [(0, 1), (1, 0)])
    slots = [block] + [move_rows(block, along_second(d)) for d in (1, 2, 3)]
    refs, send_far, send_near = run_arrange(slots, place)
    rim_far = move_rows(send_far, across)
    rim_near = lax.ppermute(send_near, "c", [(0, 1), (1, 0)])
    qs, base, res = run_middle(mine, near, far, refs, taps, flags, place)
    return run_edges(base, res, qs, refs, rim_far, rim_near, taps, flags, place)


def solution(mesh):
    split = Mesh(mesh.devices.reshape(SIZES), PB + ROW)
    specs = (P(PB + ROW, None), P(ROW + PB, None), P())
    return jax.shard_map(local, mesh=split, in_specs=specs, out_specs=P(PB, ROW), check_vma=False)
```
